128 devices in a mesh: row: 8 (over x, z_lo), col: 16 (over y, z_hi, core).
Axes of the slice: x: 4, y: 4, z: 4 (z_hi: 2, z_lo: 2; z = z_hi * 2 + z_lo), core: 2. Of those that a mesh axis runs over, the one named last changes fastest.
Arguments:
- sib_inverse: bfloat16 [24576, 12288], P('row', 'col'), may hold values from -0.0546875 to 0.0546875
- sib_panel: bfloat16 [24576, 512], P(('row', 'col')), may hold values from -0.15625 to 0.15625
- sib_cot: bfloat16 [24576, 512], P(('row', 'col')), may hold values from -6 to 6
- par_inverse: bfloat16 [16384, 16384], P('row', 'col'), may hold values from -0.046875 to 0.046875
- par_panel: bfloat16 [16384, 512], P(('row', 'col')), may hold values from -0.15625 to 0.15625
- par_cot: bfloat16 [16384, 512], P(('row', 'col')), may hold values from -6 to 6
- block_map: int32 [2, 96], replicated, may hold values from 0 to 127, as said below
- row_mask: int32 [24576], replicated, may hold values 0 or 1
Outputs:
- sib_grad: float32 [12288, 1024], P('col', 'row')
- par_grad: float32 [16384, 512], P('col', 'row')
- border_grad: float32 [16384, 16384], P('row', 'col')
The draws below stay inside these ranges and needn't reach their ends.
Inputs may be any that keep to these rules, and one draw needn't show every extreme that they name: In each row of block_map the values are distinct. Among the 24 blocks k * 24 to (k + 1) * 24 - 1 of one sibling, at most 4 have values in one range q * 16 to (q + 1) * 16 - 1, and for every k some range holds exactly 4 of them.
All inputs are finite; a program needn't handle non-finite values.
Results may differ from the reference program's by a relative error of at most 0.0003.
Values may be sent and summed in bfloat16 or wider, within the bound.
A program may use at most 128 MiB of HBM per device.

```python
import jax
import jax.numpy as jnp
from jax import lax

P_SIZE = 512
BC = 12288
BP = 16384
BLK = 128
N_ROW = 8


def draw_block_map(key, part):
    row_count = N_ROW
    half_rows = row_count // 2
    child_blocks = 2 * BC // (BLK * row_count)
    parent_blocks = BP // (BLK * row_count)
    base_load = child_blocks // row_count
    moved = base_load // 2
    sibling_maps = []
    for sibling in range(2):
        sib_key = jax.random.fold_in(key, 17 + sibling)
        rotation = jax.random.randint(jax.random.fold_in(sib_key, 1), (), 0, row_count)
        row_iota = jnp.arange(row_count, dtype=jnp.int32)
        labels = []
        for child_row in range(half_rows):
            gain_row = (child_row + rotation) % row_count
            loss_row = (child_row + rotation + half_rows) % row_count
            counts = base_load + moved * (row_iota == gain_row).astype(jnp.int32) - moved * (row_iota == loss_row).astype(jnp.int32)
            dest_rows = jnp.repeat(row_iota, counts, total_repeat_length=child_blocks)
            shuffle = jax.random.permutation(jax.random.fold_in(sib_key, 100 + child_row), child_blocks)
            labels.append(dest_rows[shuffle])
        all_dest = jnp.concatenate(labels).astype(jnp.int32)
        total = all_dest.shape[0]
        row_index = jnp.arange(total, dtype=jnp.int32)[:, None]
        col_index = jnp.arange(total, dtype=jnp.int32)[None, :]
        equal_dest = all_dest[:, None] == all_dest[None, :]
        arrival = jnp.sum((equal_dest & (col_index < row_index)).astype(jnp.int32), axis=1)
        shuffles = jnp.stack([jax.random.permutation(jax.random.fold_in(sib_key, 1000 + parent_row), parent_blocks) for parent_row in range(row_count)]).astype(jnp.int32)
        position = shuffles[all_dest, arrival]
        sibling_maps.append(all_dest * parent_blocks + position)
    return jnp.stack(sibling_maps).astype(jnp.int32)


def with_ends(drawn, own_key, least, high):
    shape = drawn.shape
    spot = [jax.random.randint(jax.random.fold_in(own_key, axis), (), 0, shape[axis]) for axis in range(len(shape))]
    drawn = drawn.at[tuple(spot)].set(least)
    longest = shape.index(max(shape))
    spot[longest] = (spot[longest] + 1) % shape[longest]
    return drawn.at[tuple(spot)].set(high)


def levels(rng, shape, cuts, smallest, largest):
    def one(axis_at, parts):
        steps = jax.random.uniform(jax.random.fold_in(jax.random.fold_in(rng, 6), axis_at), (parts,), jnp.float32, smallest / len(cuts), largest / len(cuts))
        return jnp.repeat(jnp.exp(steps), shape[axis_at] // parts).reshape((-1,) + (1,) * (len(shape) - axis_at - 1))

    gain = one(*cuts[0])
    for cut in cuts[1:]:
        gain = gain * one(*cut)
    return gain


def bell_draw(stream_key, shape, deviation, limit, cuts=(), kind=jnp.bfloat16):
    values = jax.random.normal(stream_key, shape, jnp.float32) * deviation
    if len(cuts) > 0:
        values = levels(stream_key, shape, cuts, -0.22, 0.18) * values
    return jnp.clip(values, min=-limit, max=limit).astype(kind)


def setup_inputs(seed: int = 0) -> dict:
    arg_keys = jax.random.split(jax.random.key(seed), 9)
    sib_inverse = bell_draw(arg_keys[0], (2 * BC, BC), BC ** -0.5, 0.0546875, ((0, 8), (1, 16)))
    sib_panel = bell_draw(arg_keys[1], (2 * BC, P_SIZE), (3 * P_SIZE) ** -0.5, 0.15625, ((0, 128),))
    sib_cot = bell_draw(arg_keys[2], (2 * BC, P_SIZE), 1.0, 6.0, ((0, 128),))
    par_inverse = bell_draw(arg_keys[3], (BP, BP), BP ** -0.5, 0.046875, ((0, 8), (1, 16)))
    par_panel = bell_draw(arg_keys[4], (BP, P_SIZE), (3 * P_SIZE) ** -0.5, 0.15625, ((0, 128),))
    par_cot = bell_draw(arg_keys[5], (BP, P_SIZE), 1.0, 6.0, ((0, 128),))
    block_map = draw_block_map(jax.random.fold_in(arg_keys[8], 71), 0)
    row_mask = with_ends((jax.random.randint(arg_keys[7], (2 * BC,), 0, 4) < 3).astype(jnp.int32), jax.random.fold_in(arg_keys[7], 1), 0, 1)
    return dict(sib_inverse=sib_inverse, sib_panel=sib_panel, sib_cot=sib_cot, par_inverse=par_inverse, par_panel=par_panel, par_cot=par_cot, block_map=block_map, row_mask=row_mask)


def lift_blocks(masked, block_ids):
    blocks = masked.reshape(BC // BLK, BLK, P_SIZE)
    canvas = jnp.zeros((BP // BLK, BLK, P_SIZE), masked.dtype)
    return canvas.at[block_ids.astype(jnp.int32)].set(blocks).reshape(BP, P_SIZE)


def reference(sib_inverse, sib_panel, sib_cot, par_inverse, par_panel, par_cot, block_map, row_mask):
    live = row_mask.astype(jnp.bfloat16)[:, None]
    masked_cot = sib_cot * live
    masked_panel = sib_panel * live
    contract = (((0,), (0,)), ((), ()))
    child_grads = []
    row_terms = [par_cot]
    col_terms = [par_panel]
    for sibling in range(2):
        first_row = sibling * BC
        inverse = sib_inverse[first_row:first_row + BC]
        product = -lax.dot_general(inverse, masked_cot[first_row:first_row + BC], contract, preferred_element_type=jnp.float32)
        child_grads.append(product * row_mask[first_row:first_row + BC].astype(jnp.float32)[:, None])
        row_terms.append(lift_blocks(masked_cot[first_row:first_row + BC], block_map[sibling]))
        col_terms.append(lift_blocks(masked_panel[first_row:first_row + BC], block_map[sibling]))
    sib_grad = jnp.concatenate(child_grads, axis=1)
    par_grad = -lax.dot_general(par_inverse, par_cot, contract, preferred_element_type=jnp.float32)
    row_side = jnp.concatenate(row_terms, axis=1)
    col_side = jnp.concatenate(col_terms, axis=1)
    border_grad = -lax.dot_general(row_side, col_side, (((1,), (1,)), ((), ())), preferred_element_type=jnp.float32)
    return (sib_grad, par_grad, border_grad)
```

```python
import jax
import jax.numpy as jnp
from jax import lax
from jax.experimental import pallas as pl
from jax.experimental.pallas import tpu as pltpu
from jax.sharding import PartitionSpec as P

MESH = pl.DeviceIdType.MESH
BLK = 128
G = 8
H = 256
CAP = 4
PIECE = BLK // G
TN = (((0,), (0,)), ((), ()))
NT = (((1,), (1,)), ((), ()))
SIB = 192
PAR = 128


class Gather:
    def __init__(self, slot, own, place, at, k, major, minor, sems):
        self.slot, self.own, self.place, self.at, self.k = slot, own, place, at, k
        self.m, self.n = major, minor
        self.send, self.recv, self.chip_send, self.chip_recv, self.local = sems
        self.sent = []

    def shard(self, dm, dn):
        return lax.rem(self.m + dm, 4) * 2 + (self.n if dn == 0 else 1 - self.n)

    def push(self, src, g, to):
        i = len(self.sent)
        copy = pltpu.make_async_remote_copy(
            src_ref=src,
            dst_ref=self.slot(self.k, g),
            send_sem=self.send.at[i],
            recv_sem=self.recv.at[g],
            device_id=self.at(to),
            device_id_type=MESH,
        )
        copy.start()
        self.sent.append(copy)

    def swap(self, src, g, sibling):
        pltpu.make_async_remote_copy(
            src_ref=src,
            dst_ref=self.slot(self.k, g),
            send_sem=self.chip_send.at[g],
            recv_sem=self.chip_recv.at[g],
            device_id=sibling,
            device_id_type=MESH,
        ).start()

    def wait(self, g):
        pltpu.make_async_remote_copy(
            src_ref=self.slot(self.k, g),
            dst_ref=self.slot(self.k, g),
            send_sem=self.send.at[0],
            recv_sem=self.recv.at[g],
            device_id=self.at(self.shard(0, 0)),
            device_id_type=MESH,
        ).wait_recv()

    def start(self, sibling):
        self.sibling = sibling
        me = self.shard(0, 0)
        self.push(self.own, me, self.shard(0, 1))
        self.push(self.own, me, self.shard(1, 0))
        self.push(self.own, me, self.shard(3, 0))
        self.swap(self.own, me, sibling)
        self.place(me)

    def pair(self):
        g = self.shard(0, 1)
        self.wait(g)
        self.push(self.slot(self.k, g), g, self.shard(1, 0))
        self.push(self.slot(self.k, g), g, self.shard(3, 0))
        self.swap(self.slot(self.k, g), g, self.sibling)

    def ring(self):
        g = self.shard(1, 0)
        self.wait(g)
        self.push(self.slot(self.k, g), g, self.shard(3, 0))
        self.swap(self.slot(self.k, g), g, self.sibling)
        g = self.shard(3, 0)
        self.wait(g)
        self.swap(self.slot(self.k, g), g, self.sibling)
        g = self.shard(3, 1)
        self.wait(g)
        self.push(self.slot(self.k, g), g, self.shard(1, 0))
        self.swap(self.slot(self.k, g), g, self.sibling)

    def rest(self):
        for dm, dn in ((1, 1), (2, 0), (2, 1)):
            g = self.shard(dm, dn)
            self.wait(g)
            self.swap(self.slot(self.k, g), g, self.sibling)

    def halves(self):
        for g in range(G):
            pltpu.make_async_remote_copy(
                src_ref=self.slot(1 - self.k, g),
                dst_ref=self.slot(1 - self.k, g),
                send_sem=self.chip_send.at[g],
                recv_sem=self.chip_recv.at[g],
                device_id=self.sibling,
                device_id_type=MESH,
            ).wait_recv()

    def drain(self):
        for copy in self.sent:
            copy.wait_send()
        for g in range(G):
            pltpu.make_async_remote_copy(
                src_ref=self.slot(self.k, g),
                dst_ref=self.slot(self.k, g),
                send_sem=self.chip_send.at[g],
                recv_sem=self.chip_recv.at[g],
                device_id=self.sibling,
                device_id_type=MESH,
            ).wait_send()


def exchange_kernel(
    table,
    xin,
    sib_hbm,
    par_hbm,
    pc_out,
    lc_out,
    pp_out,
    lp_out,
    sib_out,
    parg_out,
    sib_v,
    par_v,
    sc,
    pc,
    other,
    chip_sib,
    chip_par,
    pieces,
    pack_cot,
    pack_pan,
    got_cot,
    got_pan,
    turned,
    pt,
    ct,
    far,
    near_l,
    near_r,
    zs,
    zr,
    za,
    xs,
    xa,
    ag_send,
    ag_recv,
    ag_cs,
    ag_cr,
    load_sem,
    place_sem,
    x_sem,
    b_send,
    b_recv,
    c_send,
    c_recv,
    d_send,
    d_recv,
    t_sem,
    r_send,
    r_recv,
    q_send,
    q_recv,
):
    r = lax.axis_index("row")
    c = lax.axis_index("col")
    k = c % 2
    p = c // 2
    sibling = (r, p * 2 + 1 - k)

    def in_row(q):
        return (q, c)

    def in_col(q):
        return (r, q * 2 + k)

    load_sib = pltpu.make_async_copy(sib_hbm, sib_v, load_sem.at[0])
    load_par = pltpu.make_async_copy(par_hbm, par_v, load_sem.at[1])
    load_par.start()
    load_sib.start()

    barrier = pltpu.get_barrier_semaphore()
    pl.semaphore_signal(barrier, inc=1, device_id=sibling, device_id_type=MESH)
    for d in range(1, G):
        pl.semaphore_signal(barrier, inc=1, device_id=in_row(lax.rem(r + d, G)), device_id_type=MESH)
        pl.semaphore_signal(barrier, inc=1, device_id=in_col(lax.rem(p + d, G)), device_id_type=MESH)

    @pl.when(r != p)
    def _():
        pl.semaphore_signal(barrier, inc=1, device_id=(p, r * 2 + k), device_id_type=MESH)

    pl.semaphore_wait(barrier, jnp.where(r == p, 2 * G - 1, 2 * G))

    swap = pltpu.make_async_remote_copy(
        src_ref=xin.at[1 - k],
        dst_ref=other,
        send_sem=x_sem.at[0],
        recv_sem=x_sem.at[1],
        device_id=sibling,
        device_id_type=MESH,
    )
    swap.start()
    swap.wait_recv()
    first = k == 0
    for ch in range(2):
        mine, theirs = xin[k, ch * SIB : (ch + 1) * SIB], other[ch * SIB : (ch + 1) * SIB]
        low, high = jnp.where(first, mine, theirs), jnp.where(first, theirs, mine)
        chip_sib[ch, 0] = low[:BLK]
        chip_sib[ch, 1, : BLK // 2] = low[BLK:]
        chip_sib[ch, 1, BLK // 2 :] = high[: BLK // 2]
        chip_sib[ch, 2] = high[BLK // 2 :]
        at = 2 * SIB + ch * PAR
        chip_par[ch, k] = xin[k, at : at + PAR]
        chip_par[ch, 1 - k] = other[at : at + PAR]

    def sems(i):
        return ag_send.at[i], ag_recv.at[i], ag_cs.at[i], ag_cr.at[i], place_sem.at[i]

    def place_pc(me):
        pc[k, pl.ds(me * 2, 2)] = chip_par[0]

    def place_sc(me):
        sc[k, pl.ds(me * 3, 3)] = chip_sib[0]

    def placed(src, out, i):
        def place(me):
            pltpu.make_async_copy(src, out(k, me), place_sem.at[i]).start()

        return place

    def lc_slot(h, g):
        return lc_out.at[h, g]

    def lp_slot(h, g):
        return lp_out.at[h, g]

    def pp_slot(h, g):
        return pp_out.at[h, pl.ds(g * 2, 2)]

    y, zh, x, zl = p // 2, p % 2, r // 2, r % 2
    ag_pc = Gather(lambda h, g: pc.at[h, pl.ds(g * 2, 2)], chip_par.at[0], place_pc, in_col, k, y, zh, sems(0))
    ag_sc = Gather(lambda h, g: sc.at[h, pl.ds(g * 3, 3)], chip_sib.at[0], place_sc, in_col, k, y, zh, sems(1))
    ag_lc = Gather(lc_slot, got_cot, placed(got_cot, lc_slot, 0), in_col, k, y, zh, sems(2))
    ag_lp = Gather(lp_slot, got_pan, placed(got_pan, lp_slot, 1), in_row, k, x, zl, sems(3))
    ag_pp = Gather(pp_slot, turned, placed(turned, pp_slot, 2), in_row, k, x, zl, sems(4))

    turn = pltpu.make_async_remote_copy(
        src_ref=chip_par.at[1],
        dst_ref=turned,
        send_sem=t_sem.at[0],
        recv_sem=t_sem.at[1],
        device_id=(p, r * 2 + k),
        device_id_type=MESH,
    )

    b_copies = []
    for d in range(1, G):
        to = lax.rem(p + d, G)
        copy = pltpu.make_async_remote_copy(
            src_ref=chip_sib.at[:, :, pl.ds(pl.multiple_of(to * PIECE, PIECE), PIECE)],
            dst_ref=pieces.at[:, pl.ds(p * 3, 3)],
            send_sem=b_send.at[d],
            recv_sem=b_recv.at[p],
            device_id=in_col(to),
            device_id_type=MESH,
        )
        copy.start()
        b_copies.append(copy)

    @pl.when(r != p)
    def _():
        turn.start()

    @pl.when(r == p)
    def _():
        turned[...] = chip_par[1]

    ag_pc.start(sibling)
    ag_sc.start(sibling)
    pieces[:, pl.ds(p * 3, 3)] = chip_sib[:, :, pl.ds(pl.multiple_of(p * PIECE, PIECE), PIECE)]
    for d in range(1, G):
        g = lax.rem(p + d, G)
        pltpu.make_async_remote_copy(
            src_ref=pieces.at[:, pl.ds(g * 3, 3)],
            dst_ref=pieces.at[:, pl.ds(g * 3, 3)],
            send_sem=b_send.at[d],
            recv_sem=b_recv.at[g],
            device_id=in_col(g),
            device_id_type=MESH,
        ).wait_recv()

    @pl.loop(0, G)
    def _(q):
        for t in range(CAP):
            j = table[q * CAP + t]
            pack_cot[q, t] = pieces[0, j]
            pack_pan[q, t] = pieces[1, j]

    c_copies, d_copies = [], []
    for d in range(1, G):
        to = lax.rem(p + d, G)
        copy = pltpu.make_async_remote_copy(
            src_ref=pack_pan.at[to],
            dst_ref=got_pan.at[p],
            send_sem=d_send.at[d],
            recv_sem=d_recv.at[p],
            device_id=in_col(to),
            device_id_type=MESH,
        )
        copy.start()
        d_copies.append(copy)
        to = lax.rem(r + d, G)
        copy = pltpu.make_async_remote_copy(
            src_ref=pack_cot.at[to],
            dst_ref=got_cot.at[r],
            send_sem=c_send.at[d],
            recv_sem=c_recv.at[r],
            device_id=in_row(to),
            device_id_type=MESH,
        )
        copy.start()
        c_copies.append(copy)
    got_pan[p] = pack_pan[p]
    got_cot[r] = pack_cot[r]

    @pl.when(r != p)
    def _():
        turn.wait_recv()

    ag_pp.start(sibling)
    ag_pc.pair()
    for d in range(1, G):
        g = lax.rem(p + d, G)
        pltpu.make_async_remote_copy(
            src_ref=pack_pan.at[g],
            dst_ref=got_pan.at[g],
            send_sem=d_send.at[d],
            recv_sem=d_recv.at[g],
            device_id=in_col(g),
            device_id_type=MESH,
        ).wait_recv()
    ag_lp.start(sibling)
    ag_sc.pair()
    for d in range(1, G):
        g = lax.rem(r + d, G)
        pltpu.make_async_remote_copy(
            src_ref=pack_cot.at[g],
            dst_ref=got_cot.at[g],
            send_sem=c_send.at[d],
            recv_sem=c_recv.at[g],
            device_id=in_row(g),
            device_id_type=MESH,
        ).wait_recv()
    ag_lc.start(sibling)
    ag_pc.ring()
    ag_pp.pair()
    ag_lp.pair()
    ag_lc.pair()
    ag_pc.rest()
    ag_pc.halves()
    keep_pc = pltpu.make_async_copy(pc, pc_out, place_sem.at[3])
    keep_pc.start()

    load_par.wait()
    rows_p = par_v.shape[0]

    @pl.loop(0, par_v.shape[1] // 256)
    def _(i):
        at = pl.ds(pl.multiple_of(i * 256, 256), 256)
        rhs = par_v[:, at]
        for h in range(2):
            part = lax.dot_general(
                pc[h].reshape(rows_p, H), rhs, TN, preferred_element_type=jnp.float32
            )
            pt[h * 4 : (h + 1) * 4, :, at] = part.reshape(4, H // 4, 256)

    sent = []

    def give(src, dst, i, to, s, v):
        copy = pltpu.make_async_remote_copy(
            src_ref=src, dst_ref=dst, send_sem=s.at[i], recv_sem=v.at[i], device_id=to, device_id_type=MESH
        )
        copy.start()
        sent.append(copy)

    def take(dst, i, s, v):
        pltpu.make_async_remote_copy(
            src_ref=dst, dst_ref=dst, send_sem=s.at[i], recv_sem=v.at[i], device_id=sibling, device_id_type=MESH
        ).wait_recv()

    def piece(dm, dn):
        return lax.rem(x + dm, 4) * 2 + (zl if dn == 0 else 1 - zl)

    right, left, mate = in_row(piece(1, 0)), in_row(piece(3, 0)), in_row(piece(0, 1))
    give(pt.at[piece(2, 0)], far.at[0], 0, right, r_send, r_recv)
    give(pt.at[piece(2, 1)], far.at[1], 1, left, r_send, r_recv)
    give(pt.at[piece(1, 1)], near_l.at[1], 2, right, r_send, r_recv)
    give(pt.at[piece(3, 0)], near_r.at[0], 3, left, r_send, r_recv)

    ag_sc.ring()
    ag_pp.ring()
    ag_lp.ring()
    ag_lc.ring()
    ag_sc.rest()
    take(far.at[0], 0, r_send, r_recv)
    pt[piece(1, 0)] = pt[piece(1, 0)] + far[0]
    give(pt.at[piece(1, 0)], near_l.at[0], 4, right, r_send, r_recv)
    take(far.at[1], 1, r_send, r_recv)
    pt[piece(3, 1)] = pt[piece(3, 1)] + far[1]
    give(pt.at[piece(3, 1)], near_r.at[1], 5, left, r_send, r_recv)
    ag_sc.halves()

    load_sib.wait()
    rows_s = sib_v.shape[0]

    @pl.loop(0, sib_v.shape[1] // 256)
    def _(i):
        at = pl.ds(pl.multiple_of(i * 256, 256), 256)
        rhs = sib_v[:, at]
        for h in range(2):
            part = lax.dot_general(
                sc[h].reshape(rows_s, H), rhs, TN, preferred_element_type=jnp.float32
            )
            ct[h * 2 : (h + 1) * 2, :, at] = part.reshape(2, H // 2, 256)

    xb = x % 2
    beside = in_row((x + 1 - 2 * xb) * 2 + zl)
    give(ct.at[(1 - xb) * 2 + 1 - zl], za.at[1], 0, mate, q_send, q_recv)
    give(ct.at[xb * 2 + 1 - zl], za.at[0], 1, mate, q_send, q_recv)

    take(near_l.at[1], 2, r_send, r_recv)
    take(near_r.at[1], 5, r_send, r_recv)
    zs[...] = pt[piece(0, 1)] + near_l[1] + near_r[1]
    give(zs, zr, 6, mate, r_send, r_recv)

    take(za.at[1], 0, q_send, q_recv)
    xs[...] = ct[(1 - xb) * 2 + zl] + za[1]
    give(xs, xa, 2, beside, q_send, q_recv)

    ag_pp.rest()
    ag_lp.rest()
    ag_lc.rest()

    take(near_l.at[0], 4, r_send, r_recv)
    take(near_r.at[0], 3, r_send, r_recv)
    take(zr, 6, r_send, r_recv)
    parg_out[...] = pt[piece(0, 0)] + near_l[0] + near_r[0] + zr[...]
    take(za.at[0], 1, q_send, q_recv)
    take(xa, 2, q_send, q_recv)
    sib_out[...] = ct[xb * 2 + zl] + za[0] + xa[...]

    ag_pp.halves()
    ag_lp.halves()
    ag_lc.halves()

    swap.wait_send()

    @pl.when(r != p)
    def _():
        turn.wait_send()

    for copy in b_copies + c_copies + d_copies + sent:
        copy.wait_send()
    for ag in (ag_pc, ag_sc, ag_lc, ag_lp, ag_pp):
        ag.drain()
    pltpu.make_async_copy(got_cot, lc_slot(k, p), place_sem.at[0]).wait()
    pltpu.make_async_copy(got_pan, lp_slot(k, r), place_sem.at[1]).wait()
    pltpu.make_async_copy(turned, pp_slot(k, r), place_sem.at[2]).wait()
    keep_pc.wait()


def exchange(table, xin, sib_inverse, par_inverse):
    bf, f32 = jnp.bfloat16, jnp.float32
    srows, scols = sib_inverse.shape
    prows, pcols = par_inverse.shape
    anyspace = pl.BlockSpec(memory_space=pl.ANY)
    vmem = pl.BlockSpec(memory_space=pltpu.VMEM)
    dma = pltpu.SemaphoreType.DMA
    lifted = (2, G, G, CAP, PIECE, H)
    return pl.pallas_call(
        exchange_kernel,
        out_shape=(
            jax.ShapeDtypeStruct((2, 2 * G, BLK, H), bf),
            jax.ShapeDtypeStruct(lifted, bf),
            jax.ShapeDtypeStruct((2, 2 * G, BLK, H), bf),
            jax.ShapeDtypeStruct(lifted, bf),
            jax.ShapeDtypeStruct((H // 2, scols), f32),
            jax.ShapeDtypeStruct((H // 4, pcols), f32),
        ),
        in_specs=[pl.BlockSpec(memory_space=pltpu.SMEM), vmem, anyspace, anyspace],
        out_specs=(anyspace, anyspace, anyspace, anyspace, vmem, vmem),
        scratch_shapes=[
            pltpu.VMEM((srows, scols), bf),
            pltpu.VMEM((prows, pcols), bf),
            pltpu.VMEM((2, 3 * G, BLK, H), bf),
            pltpu.VMEM((2, 2 * G, BLK, H), bf),
            pltpu.VMEM((2 * (SIB + PAR), H), bf),
            pltpu.VMEM((2, 3, BLK, H), bf),
            pltpu.VMEM((2, 2, BLK, H), bf),
            pltpu.VMEM((2, 3 * G, PIECE, H), bf),
            pltpu.VMEM((G, CAP, PIECE, H), bf),
            pltpu.VMEM((G, CAP, PIECE, H), bf),
            pltpu.VMEM((G, CAP, PIECE, H), bf),
            pltpu.VMEM((G, CAP, PIECE, H), bf),
            pltpu.VMEM((2, BLK, H), bf),
            pltpu.VMEM((8, H // 4, pcols), f32),
            pltpu.VMEM((4, H // 2, scols), f32),
            pltpu.VMEM((2, H // 4, pcols), f32),
            pltpu.VMEM((2, H // 4, pcols), f32),
            pltpu.VMEM((2, H // 4, pcols), f32),
            pltpu.VMEM((H // 4, pcols), f32),
            pltpu.VMEM((H // 4, pcols), f32),
            pltpu.VMEM((2, H // 2, scols), f32),
            pltpu.VMEM((H // 2, scols), f32),
            pltpu.VMEM((H // 2, scols), f32),
            dma((5, 8)),
            dma((5, 8)),
            dma((5, 8)),
            dma((5, 8)),
            dma((2,)),
            dma((5,)),
            dma((2,)),
            dma((8,)),
            dma((8,)),
            dma((8,)),
            dma((8,)),
            dma((8,)),
            dma((8,)),
            dma((2,)),
            dma((7,)),
            dma((7,)),
            dma((3,)),
            dma((3,)),
        ],
        compiler_params=pltpu.CompilerParams(
            collective_id=0, has_side_effects=True, vmem_limit_bytes=50 << 20
        ),
    )(table, xin, sib_inverse, par_inverse)


def border_kernel(row_tab, col_tab, pc, a00, a01, a10, a11, pp, lp, out, left, right):
    i = pl.program_id(0)

    @pl.when(i == 0)
    def _():
        for b in range(8):
            rows = slice(b * BLK, (b + 1) * BLK)
            for h in range(2):
                right[rows, h * H : (h + 1) * H] = pp[h, b]
            for s in range(2):
                slot = col_tab[s * 8 + b]
                live = slot >= 0
                at = jnp.maximum(slot, 0)
                for h in range(2):
                    lanes = slice((1 + s) * 2 * H + h * H, (1 + s) * 2 * H + (h + 1) * H)
                    block = lp[h, at // CAP, :, at % CAP].reshape(BLK, H)
                    right[rows, lanes] = jnp.where(live, block, jnp.zeros_like(block))

    for b in range(2):
        rows = slice(b * BLK, (b + 1) * BLK)
        for h in range(2):
            left[rows, h * H : (h + 1) * H] = pc[h, b]
        for s, ref in enumerate(((a00, a01)[b], (a10, a11)[b])):
            live = row_tab[s * 16 + i * 2 + b] >= 0
            for h in range(2):
                lanes = slice((1 + s) * 2 * H + h * H, (1 + s) * 2 * H + (h + 1) * H)
                block = ref[h, :, 0].reshape(BLK, H)
                left[rows, lanes] = jnp.where(live, block, jnp.zeros_like(block))
    out[...] = lax.dot_general(left[...], right[...], NT, preferred_element_type=jnp.float32)


def border(row_tab, col_tab, half, pc, lc, pp, lp):
    rows = 2 * G * BLK
    cols = G * BLK
    lc = lc.reshape(2, G, G * CAP, PIECE, H)

    def slot_spec(s, b):
        return pl.BlockSpec(
            (2, G, 1, PIECE, H),
            lambda i, rt, ct, hf: (0, 0, jnp.maximum(rt[s * 16 + i * 2 + b], 0), 0, 0),
        )

    def body(rt, ct, hf, *refs):
        border_kernel(rt, ct, *refs)

    return pl.pallas_call(
        body,
        out_shape=jax.ShapeDtypeStruct((rows, cols), jnp.float32),
        grid_spec=pltpu.PrefetchScalarGridSpec(
            num_scalar_prefetch=3,
            grid=(G,),
            in_specs=[
                pl.BlockSpec((2, 2, BLK, H), lambda i, rt, ct, hf: (0, i, 0, 0)),
                slot_spec(0, 0),
                slot_spec(0, 1),
                slot_spec(1, 0),
                slot_spec(1, 1),
                pl.BlockSpec((2, 8, BLK, H), lambda i, rt, ct, hf: (0, hf[0], 0, 0)),
                pl.BlockSpec((2, G, G, CAP, PIECE, H), lambda i, rt, ct, hf: (0, 0, 0, 0, 0, 0)),
            ],
            out_specs=pl.BlockSpec((2 * BLK, cols), lambda i, rt, ct, hf: (i, 0)),
            scratch_shapes=[
                pltpu.VMEM((2 * BLK, 6 * H), jnp.bfloat16),
                pltpu.VMEM((cols, 6 * H), jnp.bfloat16),
            ],
        ),
        compiler_params=pltpu.CompilerParams(vmem_limit_bytes=50 << 20),
    )(row_tab, col_tab, half, pc, lc, lc, lc, lc, pp, lp)


def on_device(sib_inverse, sib_panel, sib_cot, par_inverse, par_panel, par_cot, block_map, row_mask):
    r = lax.axis_index("row")
    c = lax.axis_index("col")
    tile_cols = sib_inverse.shape[1]
    half_rows = G // 2
    tile_blocks = 3 * G
    parent_blocks = 2 * G

    live = lax.dynamic_slice_in_dim(row_mask, (r * 16 + c) * SIB, SIB).astype(jnp.bfloat16)[:, None]
    xin = jnp.concatenate([sib_cot * live, -(sib_panel * live), par_cot, -par_panel], axis=0)
    xin = xin.reshape(-1, 2, H).transpose(1, 0, 2)

    ids = block_map.reshape(G, tile_blocks)
    dest = ids // parent_blocks
    iota = jnp.arange(tile_blocks, dtype=jnp.int32)
    before = (dest[:, :, None] == dest[:, None, :]) & (iota[None, None, :] < iota[None, :, None])
    rank = jnp.sum(before.astype(jnp.int32), axis=-1)
    mine = lax.dynamic_index_in_dim(dest * CAP + rank, r, 0, keepdims=False)
    slots = jnp.arange(G * CAP, dtype=jnp.int32)
    table = jnp.sum(jnp.where(mine[None, :] == slots[:, None], iota[None, :], 0), axis=1)

    held = (jnp.arange(G, dtype=jnp.int32)[:, None] * CAP + rank).reshape(2, -1)
    flat = block_map.reshape(2, -1)

    def lookup(first, count):
        want = first + jnp.arange(count, dtype=jnp.int32)
        hit = flat[:, None, :] == want[None, :, None]
        return (jnp.sum(jnp.where(hit, held[:, None, :] + 1, 0), axis=-1) - 1).reshape(-1)

    row_tab = lookup(r * parent_blocks, parent_blocks)
    col_tab = lookup(c * G, G)

    pc, lc, pp, lp, sib_sum, par_sum = exchange(table, xin, sib_inverse, par_inverse)
    border_grad = border(row_tab, col_tab, (c % 2).reshape(1), pc, lc, pp, lp)

    live_cols = lax.dynamic_slice_in_dim(
        row_mask, (r // half_rows) * (tile_cols * 16) + c * tile_cols, tile_cols
    ).astype(jnp.float32)
    return (-(sib_sum * live_cols[None, :]).T, -par_sum.T, border_grad)


def solution(mesh):
    placed = (
        P("row", "col"),
        P(("row", "col"), None),
        P(("row", "col"), None),
        P("row", "col"),
        P(("row", "col"), None),
        P(("row", "col"), None),
        P(),
        P(),
    )
    return jax.shard_map(
        on_device,
        mesh=mesh,
        in_specs=placed,
        out_specs=(P("col", "row"), P("col", "row"), P("row", "col")),
        check_vma=False,
    )
```

```python
import jax
import jax.numpy as jnp
from jax import lax
from jax.experimental import pallas as pl
from jax.experimental.pallas import tpu as pltpu
from jax.sharding import PartitionSpec as P

MESH = pl.DeviceIdType.MESH
BLK = 128
G = 8
H = 256
CAP = 4
PIECE = BLK // G
TN = (((0,), (0,)), ((), ()))
NT = (((1,), (1,)), ((), ()))
SIB = 192
PAR = 128
ROW_TAB, COL_TAB, END = 32, 64, 80


class Gather:
    def __init__(self, slot, own, place, at, k, major, minor, sems):
        self.slot, self.own, self.place, self.at, self.k = slot, own, place, at, k
        self.m, self.n = major, minor
        self.send, self.recv, self.chip_send, self.chip_recv = sems
        self.sent = []

    def shard(self, dm, dn):
        return lax.rem(self.m + dm, 4) * 2 + (self.n if dn == 0 else 1 - self.n)

    def push(self, src, g, to):
        i = len(self.sent)
        copy = pltpu.make_async_remote_copy(
            src_ref=src,
            dst_ref=self.slot(self.k, g),
            send_sem=self.send.at[i],
            recv_sem=self.recv.at[g],
            device_id=self.at(to),
            device_id_type=MESH,
        )
        copy.start()
        self.sent.append(copy)

    def swap(self, src, g, sibling):
        pltpu.make_async_remote_copy(
            src_ref=src,
            dst_ref=self.slot(self.k, g),
            send_sem=self.chip_send.at[g],
            recv_sem=self.chip_recv.at[g],
            device_id=sibling,
            device_id_type=MESH,
        ).start()

    def wait(self, g):
        pltpu.make_async_remote_copy(
            src_ref=self.slot(self.k, g),
            dst_ref=self.slot(self.k, g),
            send_sem=self.send.at[0],
            recv_sem=self.recv.at[g],
            device_id=self.at(self.shard(0, 0)),
            device_id_type=MESH,
        ).wait_recv()

    def start(self, sibling):
        self.sibling = sibling
        me = self.shard(0, 0)
        self.push(self.own, me, self.shard(0, 1))
        self.push(self.own, me, self.shard(1, 0))
        self.push(self.own, me, self.shard(3, 0))
        self.swap(self.own, me, sibling)
        self.place(me)

    def pair(self):
        g = self.shard(0, 1)
        self.wait(g)
        self.push(self.slot(self.k, g), g, self.shard(1, 0))
        self.push(self.slot(self.k, g), g, self.shard(3, 0))
        self.swap(self.slot(self.k, g), g, self.sibling)

    def ring(self):
        g = self.shard(1, 0)
        self.wait(g)
        self.push(self.slot(self.k, g), g, self.shard(3, 0))
        self.swap(self.slot(self.k, g), g, self.sibling)
        g = self.shard(3, 0)
        self.wait(g)
        self.swap(self.slot(self.k, g), g, self.sibling)
        g = self.shard(3, 1)
        self.wait(g)
        self.push(self.slot(self.k, g), g, self.shard(1, 0))
        self.swap(self.slot(self.k, g), g, self.sibling)

    def rest(self):
        for dm, dn in ((1, 1), (2, 0), (2, 1)):
            g = self.shard(dm, dn)
            self.wait(g)
            self.swap(self.slot(self.k, g), g, self.sibling)

    def halves(self):
        for g in range(G):
            pltpu.make_async_remote_copy(
                src_ref=self.slot(1 - self.k, g),
                dst_ref=self.slot(1 - self.k, g),
                send_sem=self.chip_send.at[g],
                recv_sem=self.chip_recv.at[g],
                device_id=self.sibling,
                device_id_type=MESH,
            ).wait_recv()

    def drain(self):
        for copy in self.sent:
            copy.wait_send()
        for g in range(G):
            pltpu.make_async_remote_copy(
                src_ref=self.slot(self.k, g),
                dst_ref=self.slot(self.k, g),
                send_sem=self.chip_send.at[g],
                recv_sem=self.chip_recv.at[g],
                device_id=self.sibling,
                device_id_type=MESH,
            ).wait_send()


STEP = 4


def exchange_kernel(
    tab,
    mask_hbm,
    sib_cot_hbm,
    sib_panel_hbm,
    par_cot_hbm,
    par_panel_hbm,
    sib_hbm,
    par_hbm,
    part_out,
    lc_out,
    lp_out,
    sib_out,
    parg_out,
    mask,
    sib_cot,
    sib_panel,
    par_panel,
    sib_v,
    par_v,
    sc,
    pc,
    pp,
    mcol,
    halves,
    other,
    halves_p,
    other_p,
    chip_sib,
    chip_par,
    pieces,
    par_pieces,
    pack_cot,
    pack_pan,
    got_cot,
    got_pan,
    got_par,
    pt,
    ct,
    far,
    near_l,
    near_r,
    zs,
    zr,
    s_in,
    s_mid,
    s_last,
    pmat,
    tiles,
    ag_send,
    ag_recv,
    ag_cs,
    ag_cr,
    load_sem,
    place_sem,
    tile_sem,
    x_sem,
    b_send,
    b_recv,
    e_send,
    e_recv,
    c_send,
    c_recv,
    d_send,
    d_recv,
    f_send,
    f_recv,
    r_send,
    r_recv,
    q_send,
    q_recv,
):
    r = lax.axis_index("row")
    c = lax.axis_index("col")
    k = c % 2
    p = c // 2
    y, zh, x, zl = p // 2, p % 2, r // 2, r % 2
    sibling = (r, p * 2 + 1 - k)
    started = []

    def in_row(q):
        return (q, c)

    def in_col(q):
        return (r, q * 2 + k)

    def remote(src, dst, send, recv, to):
        return pltpu.make_async_remote_copy(
            src_ref=src, dst_ref=dst, send_sem=send, recv_sem=recv, device_id=to, device_id_type=MESH
        )

    def give(src, dst, send, recv, to):
        copy = remote(src, dst, send, recv, to)
        copy.start()
        started.append(copy)

    def take(dst, send, recv):
        remote(dst, dst, send, recv, sibling).wait_recv()

    def each(dst, at, me, send, recv):
        for d in range(1, G):
            g = lax.rem(me + d, G)
            take(dst.at[at(g)], send.at[d], recv.at[g])

    barrier = pltpu.get_barrier_semaphore()
    pl.semaphore_signal(barrier, inc=1, device_id=sibling, device_id_type=MESH)
    for d in range(1, G):
        pl.semaphore_signal(barrier, inc=1, device_id=in_row(lax.rem(r + d, G)), device_id_type=MESH)
        pl.semaphore_signal(barrier, inc=1, device_id=in_col(lax.rem(p + d, G)), device_id_type=MESH)
    loads = [
        pltpu.make_async_copy(src, dst, load_sem.at[i])
        for i, (src, dst) in enumerate(
            (
                (par_panel_hbm, par_panel),
                (par_cot_hbm, pc.at[c]),
                (mask_hbm, mask),
                (sib_cot_hbm, sib_cot),
                (sib_panel_hbm, sib_panel),
                (par_hbm, par_v),
                (sib_hbm, sib_v),
            )
        )
    ]
    for load in loads:
        load.start()

    def sems(i):
        return ag_send.at[i], ag_recv.at[i], ag_cs.at[i], ag_cr.at[i]

    def nothing(me):
        pass

    def placed(src, out, i):
        def place(me):
            pltpu.make_async_copy(src, out(k, me), place_sem.at[i]).start()

        return place

    def place_pp(me):
        pp[k, me] = got_par[...]

    def lc_slot(h, g):
        return lc_out.at[h, g]

    def lp_slot(h, g):
        return lp_out.at[h, g]

    ag_pc = Gather(lambda h, g: pc.at[g * 2 + h], pc.at[c], nothing, in_col, k, y, zh, sems(0))
    ag_sc = Gather(lambda h, g: sc.at[g * 2 + h], sc.at[c], nothing, in_col, k, y, zh, sems(1))
    ag_lc = Gather(lc_slot, got_cot, placed(got_cot, lc_slot, 0), in_col, k, y, zh, sems(2))
    ag_lp = Gather(lp_slot, got_pan, placed(got_pan, lp_slot, 1), in_row, k, x, zl, sems(3))
    ag_pp = Gather(lambda h, g: pp.at[h, g], got_par, place_pp, in_row, k, x, zl, sems(4))

    loads[0].wait()
    for h in range(2):
        halves_p[h] = par_panel[:, h * H : (h + 1) * H]
    loads[1].wait()
    pl.semaphore_wait(barrier, 2 * G - 1)
    give(halves_p.at[1 - k], other_p, x_sem.at[0], x_sem.at[1], sibling)
    ag_pc.start(sibling)

    for load in loads[2:5]:
        load.wait()
    line = (r * 16 + c) * 3 // 2
    for i in range(2):
        row = mask[pl.ds(line + i, 1), :].astype(jnp.float32)
        mcol[i * BLK : (i + 1) * BLK] = jnp.broadcast_to(row, (BLK, BLK)).T.astype(jnp.bfloat16)
    live = mcol[pl.ds(pl.multiple_of(k * 64, 64), SIB)]
    for h in range(2):
        for i in range(2):
            lanes = slice(h * H + i * BLK, h * H + (i + 1) * BLK)
            cot = sib_cot[:, lanes] * live
            sc[c, :, lanes] = cot
            halves[h, :SIB, i * BLK : (i + 1) * BLK] = cot
            halves[h, SIB:, i * BLK : (i + 1) * BLK] = sib_panel[:, lanes] * live
    give(halves.at[1 - k], other, x_sem.at[2], x_sem.at[3], sibling)

    def strip(i):
        return pl.ds(pl.multiple_of(i * PIECE, PIECE), PIECE)

    take(other_p, x_sem.at[0], x_sem.at[1])
    chip_par[k] = halves_p[k]
    chip_par[1 - k] = other_p[...]
    for d in range(1, G):
        to = lax.rem(r + d, G)
        give(chip_par.at[:, strip(to)], par_pieces.at[r], e_send.at[d], e_recv.at[r], in_row(to))
    par_pieces[r] = chip_par[:, strip(r)]

    take(other, x_sem.at[2], x_sem.at[3])
    first = k == 0
    for ch in range(2):
        mine, theirs = halves[k, ch * SIB : (ch + 1) * SIB], other[ch * SIB : (ch + 1) * SIB]
        low, high = jnp.where(first, mine, theirs), jnp.where(first, theirs, mine)
        chip_sib[ch, 0] = low[:BLK]
        chip_sib[ch, 1, : BLK // 2] = low[BLK:]
        chip_sib[ch, 1, BLK // 2 :] = high[: BLK // 2]
        chip_sib[ch, 2] = high[BLK // 2 :]
    for d in range(1, G):
        to = lax.rem(p + d, G)
        give(chip_sib.at[:, :, strip(to)], pieces.at[:, pl.ds(p * 3, 3)], b_send.at[d], b_recv.at[p], in_col(to))
    pieces[:, pl.ds(p * 3, 3)] = chip_sib[:, :, strip(p)]

    each(par_pieces, lambda g: g, r, e_send, e_recv)
    for d in range(1, G):
        to = lax.rem(p + d, G)
        give(par_pieces.at[to], got_par.at[p], f_send.at[d], f_recv.at[p], in_col(to))
    got_par[p] = par_pieces[p]

    ag_pc.pair()
    for d in range(1, G):
        g = lax.rem(p + d, G)
        take(pieces.at[:, pl.ds(g * 3, 3)], b_send.at[d], b_recv.at[g])

    @pl.loop(0, G)
    def _(q):
        for t in range(CAP):
            j = tab[q * CAP + t]
            pack_cot[q, t] = pieces[0, j]
            pack_pan[q, t] = pieces[1, j]

    for d in range(1, G):
        to = lax.rem(p + d, G)
        give(pack_pan.at[to], got_pan.at[p], d_send.at[d], d_recv.at[p], in_col(to))
    for d in range(1, G):
        to = lax.rem(r + d, G)
        give(pack_cot.at[to], got_cot.at[r], c_send.at[d], c_recv.at[r], in_row(to))
    got_pan[p] = pack_pan[p]
    got_cot[r] = pack_cot[r]

    each(got_par, lambda g: g, p, f_send, f_recv)
    ag_pp.start(sibling)
    ag_pc.ring()
    each(got_pan, lambda g: g, p, d_send, d_recv)
    ag_lp.start(sibling)
    each(got_cot, lambda g: g, r, c_send, c_recv)
    ag_lc.start(sibling)
    ag_pc.rest()
    ag_pp.pair()
    ag_pc.halves()

    loads[5].wait()
    rows_p = par_v.shape[0]

    @pl.loop(0, par_v.shape[1] // 256)
    def _(i):
        at = pl.ds(pl.multiple_of(i * 256, 256), 256)
        part = lax.dot_general(
            pc[...].reshape(rows_p, 2 * H), par_v[:, at], TN, preferred_element_type=jnp.float32
        )
        pt[:, :, at] = part.reshape(8, H // 4, 256)

    def piece(dm, dn):
        return lax.rem(x + dm, 4) * 2 + (zl if dn == 0 else 1 - zl)

    right, left, mate = in_row(piece(1, 0)), in_row(piece(3, 0)), in_row(piece(0, 1))

    def r_give(src, dst, i, to):
        give(src, dst, r_send.at[i], r_recv.at[i], to)

    def r_take(dst, i):
        take(dst, r_send.at[i], r_recv.at[i])

    def q_give(src, dst, i, to):
        give(src, dst, q_send.at[i], q_recv.at[i], to)

    def q_take(dst, i):
        take(dst, q_send.at[i], q_recv.at[i])

    r_give(pt.at[piece(2, 0)], far.at[0], 0, right)
    r_give(pt.at[piece(2, 1)], far.at[1], 1, left)
    r_give(pt.at[piece(1, 1)], near_l.at[1], 2, right)
    r_give(pt.at[piece(3, 0)], near_r.at[0], 3, left)

    ag_sc.start(sibling)
    ag_lp.pair()
    ag_lc.pair()
    ag_pp.ring()
    ag_sc.pair()

    r_take(far.at[0], 0)
    pt[piece(1, 0)] = pt[piece(1, 0)] + far[0]
    r_give(pt.at[piece(1, 0)], near_l.at[0], 4, right)
    r_take(far.at[1], 1)
    pt[piece(3, 1)] = pt[piece(3, 1)] + far[1]
    r_give(pt.at[piece(3, 1)], near_r.at[1], 5, left)

    ag_sc.ring()
    ag_lc.ring()
    ag_sc.rest()
    ag_sc.halves()

    loads[6].wait()
    rows_s, cols_s = sib_v.shape
    cut = cols_s // 3 * 2
    parts = (slice(0, cut), slice(cut, cols_s))
    xb = x % 2
    beside = in_row((x + 1 - 2 * xb) * 2 + zl)
    own, by_z, by_x, by_xz = xb * 2 + zl, xb * 2 + 1 - zl, (1 - xb) * 2 + zl, (1 - xb) * 2 + 1 - zl

    def sib_part(i):
        part = lax.dot_general(
            sc[...].reshape(rows_s, 2 * H), sib_v[:, parts[i]], TN, preferred_element_type=jnp.float32
        )
        ct[:, :, parts[i]] = part.reshape(4, H // 2, -1)

    sib_part(0)
    q_give(ct.at[by_xz, :, parts[0]], s_in.at[1, :, parts[0]], 0, mate)
    q_give(ct.at[by_z, :, parts[0]], s_in.at[0, :, parts[0]], 1, mate)
    sib_part(1)
    q_give(ct.at[by_xz, :, parts[1]], s_in.at[1, :, parts[1]], 2, beside)
    q_give(ct.at[by_x, :, parts[1]], s_in.at[0, :, parts[1]], 3, beside)

    ag_lp.ring()
    ag_pp.rest()

    r_take(near_l.at[1], 2)
    r_take(near_r.at[1], 5)
    zs[...] = pt[piece(0, 1)] + near_l[1] + near_r[1]
    r_give(zs, zr, 6, mate)

    ag_pp.halves()
    for n in range(8):
        rows = slice(n * BLK, (n + 1) * BLK)
        for h in range(2):
            pmat[rows, h * H : (h + 1) * H] = pp[h, :, 4 * k + n // 2, n % 2].reshape(BLK, H)
    rows_t = STEP * BLK
    stores = []

    def tile(t):
        if t >= 2:
            stores[t - 2].wait()
        tiles[t % 2] = lax.dot_general(
            pc[t * STEP : (t + 1) * STEP].reshape(rows_t, 2 * H),
            pmat[...],
            NT,
            preferred_element_type=jnp.float32,
        )
        stores.append(
            pltpu.make_async_copy(tiles.at[t % 2], part_out.at[t * rows_t : (t + 1) * rows_t], tile_sem.at[t % 2])
        )
        stores[t].start()

    tile(0)
    q_take(s_in.at[1, :, parts[1]], 2)
    s_mid[:, parts[1]] = ct[by_z, :, parts[1]] + s_in[1, :, parts[1]]
    q_give(s_mid.at[:, parts[1]], s_last.at[:, parts[1]], 5, mate)
    tile(1)
    q_take(s_in.at[1, :, parts[0]], 0)
    s_mid[:, parts[0]] = ct[by_x, :, parts[0]] + s_in[1, :, parts[0]]
    q_give(s_mid.at[:, parts[0]], s_last.at[:, parts[0]], 4, beside)
    tile(2)
    ag_lc.rest()
    ag_lp.rest()
    tile(3)

    r_take(near_l.at[0], 4)
    r_take(near_r.at[0], 3)
    r_take(zr, 6)
    parg_out[...] = -(pt[piece(0, 0)] + near_l[0] + near_r[0] + zr[...])
    q_take(s_in.at[0, :, parts[0]], 1)
    q_take(s_in.at[0, :, parts[1]], 3)
    q_take(s_last.at[:, parts[0]], 4)
    q_take(s_last.at[:, parts[1]], 5)
    first_line = (x // 2) * (mask.shape[0] // 2) + c * (cols_s // BLK)
    for j in range(cols_s // BLK):
        lanes = slice(j * BLK, (j + 1) * BLK)
        keep = mask[pl.ds(first_line + j, 1), :].astype(jnp.float32)
        sib_out[:, lanes] = -(ct[own, :, lanes] + s_in[0, :, lanes] + s_last[:, lanes]) * keep

    ag_lc.halves()
    ag_lp.halves()

    for copy in started:
        copy.wait_send()
    for ag in (ag_pc, ag_sc, ag_lc, ag_lp, ag_pp):
        ag.drain()
    pltpu.make_async_copy(got_cot, lc_slot(k, p), place_sem.at[0]).wait()
    pltpu.make_async_copy(got_pan, lp_slot(k, r), place_sem.at[1]).wait()
    stores[-2].wait()
    stores[-1].wait()


def exchange(tab, mask, sib_cot, sib_panel, par_cot, par_panel, sib_inverse, par_inverse):
    bf, f32 = jnp.bfloat16, jnp.float32
    srows, scols = sib_inverse.shape
    prows, pcols = par_inverse.shape
    anyspace = pl.BlockSpec(memory_space=pl.ANY)
    vmem = pl.BlockSpec(memory_space=pltpu.VMEM)
    dma = pltpu.SemaphoreType.DMA
    lifted = jax.ShapeDtypeStruct((2, G, G, CAP, PIECE, H), bf)
    return pl.pallas_call(
        exchange_kernel,
        out_shape=(
            jax.ShapeDtypeStruct((prows, pcols), f32),
            lifted,
            lifted,
            jax.ShapeDtypeStruct((H // 2, scols), f32),
            jax.ShapeDtypeStruct((H // 4, pcols), f32),
        ),
        in_specs=[pl.BlockSpec(memory_space=pltpu.SMEM)] + [anyspace] * 7,
        out_specs=(anyspace, anyspace, anyspace, vmem, vmem),
        scratch_shapes=[
            pltpu.VMEM(mask.shape, jnp.int32),
            pltpu.VMEM((SIB, 2 * H), bf),
            pltpu.VMEM((SIB, 2 * H), bf),
            pltpu.VMEM((PAR, 2 * H), bf),
            pltpu.VMEM((srows, scols), bf),
            pltpu.VMEM((prows, pcols), bf),
            pltpu.VMEM((2 * G, SIB, 2 * H), bf),
            pltpu.VMEM((2 * G, PAR, 2 * H), bf),
            pltpu.VMEM((2, G, G, 2, PIECE, H), bf),
            pltpu.VMEM((2 * BLK, BLK), bf),
            pltpu.VMEM((2, 2 * SIB, H), bf),
            pltpu.VMEM((2 * SIB, H), bf),
            pltpu.VMEM((2, PAR, H), bf),
            pltpu.VMEM((PAR, H), bf),
            pltpu.VMEM((2, 3, BLK, H), bf),
            pltpu.VMEM((2, BLK, H), bf),
            pltpu.VMEM((2, 3 * G, PIECE, H), bf),
            pltpu.VMEM((G, 2, PIECE, H), bf),
            pltpu.VMEM((G, CAP, PIECE, H), bf),
            pltpu.VMEM((G, CAP, PIECE, H), bf),
            pltpu.VMEM((G, CAP, PIECE, H), bf),
            pltpu.VMEM((G, CAP, PIECE, H), bf),
            pltpu.VMEM((G, 2, PIECE, H), bf),
            pltpu.VMEM((8, H // 4, pcols), f32),
            pltpu.VMEM((4, H // 2, scols), f32),
            pltpu.VMEM((2, H // 4, pcols), f32),
            pltpu.VMEM((2, H // 4, pcols), f32),
            pltpu.VMEM((2, H // 4, pcols), f32),
            pltpu.VMEM((H // 4, pcols), f32),
            pltpu.VMEM((H // 4, pcols), f32),
            pltpu.VMEM((2, H // 2, scols), f32),
            pltpu.VMEM((H // 2, scols), f32),
            pltpu.VMEM((H // 2, scols), f32),
            pltpu.VMEM((pcols, 2 * H), bf),
            pltpu.VMEM((2, STEP * BLK, pcols), f32),
            dma((5, 8)),
            dma((5, 8)),
            dma((5, 8)),
            dma((5, 8)),
            dma((7,)),
            dma((2,)),
            dma((2,)),
            dma((4,)),
            *[dma((8,))] * 10,
            dma((7,)),
            dma((7,)),
            dma((6,)),
            dma((6,)),
        ],
        compiler_params=pltpu.CompilerParams(
            collective_id=0, has_side_effects=True, vmem_limit_bytes=54 << 20
        ),
    )(tab, mask, sib_cot, sib_panel, par_cot, par_panel, sib_inverse, par_inverse)


def border_kernel(tab, part, *refs):
    lifted, panels, (out, left, right) = refs[: 2 * STEP], refs[2 * STEP : 2 * STEP + 16], refs[2 * STEP + 16 :]
    i = pl.program_id(0)

    def lanes(s, h):
        return slice((2 * s + h) * H, (2 * s + h + 1) * H)

    @pl.when(i == 0)
    def _():
        for b in range(8):
            rows = slice(b * BLK, (b + 1) * BLK)
            for h in range(2):
                for s in range(2):
                    block = panels[s * 8 + b][h, 0, :, 0].reshape(BLK, H)
                    there = tab[COL_TAB + s * 8 + b] >= 0
                    right[rows, lanes(s, h)] = jnp.where(there, block, jnp.zeros_like(block))

    for b in range(STEP):
        rows = slice(b * BLK, (b + 1) * BLK)
        for s in range(2):
            there = tab[ROW_TAB + s * 16 + i * STEP + b] >= 0
            for h in range(2):
                block = lifted[s * STEP + b][h, :, 0].reshape(BLK, H)
                left[rows, lanes(s, h)] = jnp.where(there, block, jnp.zeros_like(block))
    out[...] = -(part[...] + lax.dot_general(left[...], right[...], NT, preferred_element_type=jnp.float32))


def border(tab, part, lc, lp):
    rows, cols = part.shape
    lc = lc.reshape(2, G, G * CAP, PIECE, H)

    def lifted_spec(s, b):
        return pl.BlockSpec(
            (2, G, 1, PIECE, H),
            lambda i, t: (0, 0, jnp.maximum(t[ROW_TAB + s * 16 + i * STEP + b], 0), 0, 0),
        )

    def panel_spec(n):
        def at(i, t):
            slot = jnp.maximum(t[COL_TAB + n], 0)
            return 0, slot // CAP, 0, slot % CAP, 0, 0

        return pl.BlockSpec((2, 1, G, 1, PIECE, H), at, pipeline_mode=pl.Buffered(1))

    return pl.pallas_call(
        border_kernel,
        out_shape=jax.ShapeDtypeStruct((rows, cols), jnp.float32),
        grid_spec=pltpu.PrefetchScalarGridSpec(
            num_scalar_prefetch=1,
            grid=(2 * G // STEP,),
            in_specs=[pl.BlockSpec((STEP * BLK, cols), lambda i, t: (i, 0))]
            + [lifted_spec(s, b) for s in range(2) for b in range(STEP)]
            + [panel_spec(n) for n in range(16)],
            out_specs=pl.BlockSpec((STEP * BLK, cols), lambda i, t: (i, 0)),
            scratch_shapes=[
                pltpu.VMEM((STEP * BLK, 4 * H), jnp.bfloat16),
                pltpu.VMEM((cols, 4 * H), jnp.bfloat16),
            ],
        ),
        compiler_params=pltpu.CompilerParams(vmem_limit_bytes=50 << 20),
    )(tab, part, *([lc] * (2 * STEP)), *([lp] * 16))


def tables(block_map, r, c):
    blocks = 3 * G
    tile_blocks = 2 * G
    ids = block_map.reshape(G, blocks)
    dest = ids // tile_blocks
    iota = jnp.arange(blocks, dtype=jnp.int32)
    tile = jnp.arange(G, dtype=jnp.int32)[:, None]
    before = (dest[:, :, None] == dest[:, None, :]) & (iota[None, None, :] < iota[None, :, None])
    rank = jnp.sum(before.astype(jnp.int32), axis=-1)
    n = jnp.arange(END, dtype=jnp.int32)[:, None, None]
    slot = dest * CAP + rank
    in_slot = (n < ROW_TAB) & (tile == r)[None] & (slot[None] == n)
    s, row_at, col_at = tile // (G // 2), n - ROW_TAB, n - COL_TAB
    in_rows = (n >= ROW_TAB) & (n < COL_TAB) & (s[None] == row_at // 16) & (ids[None] == r * 16 + row_at % 16)
    in_cols = (n >= COL_TAB) & (n < END) & (s[None] == col_at // 8) & (ids[None] == c * 8 + col_at % 8)
    value = jnp.where(in_slot, iota[None, None], 0) + jnp.where(in_rows | in_cols, (tile * CAP + rank + 1)[None], 0)
    flat = n[:, 0, 0]
    return jnp.sum(value, axis=(1, 2)) + jnp.where(flat < ROW_TAB, 0, -1)


def on_device(sib_inverse, sib_panel, sib_cot, par_inverse, par_panel, par_cot, block_map, row_mask):
    r = lax.axis_index("row")
    c = lax.axis_index("col")
    tab = tables(block_map, r, c)
    mask = row_mask.reshape(-1, BLK)
    part, lc, lp, sib_sum, par_sum = exchange(
        tab, mask, sib_cot, sib_panel, par_cot, par_panel, sib_inverse, par_inverse
    )
    return sib_sum.T, par_sum.T, border(tab, part, lc, lp)


def solution(mesh):
    placed = (
        P("row", "col"),
        P(("row", "col"), None),
        P(("row", "col"), None),
        P("row", "col"),
        P(("row", "col"), None),
        P(("row", "col"), None),
        P(),
        P(),
    )
    return jax.shard_map(
        on_device,
        mesh=mesh,
        in_specs=placed,
        out_specs=(P("col", "row"), P("col", "row"), P("row", "col")),
        check_vma=False,
    )
```

```python
import jax
import jax.numpy as jnp
from jax import lax
from jax.experimental import pallas as pl
from jax.experimental.pallas import tpu as pltpu
from jax.sharding import PartitionSpec as P

MESH = pl.DeviceIdType.MESH
BLK = 128
G = 8
H = 256
CAP = 4
PIECE = BLK // G
TN = (((0,), (0,)), ((), ()))
NT = (((1,), (1,)), ((), ()))
SIB = 192
PAR = 128
ROW_TAB, COL_TAB, END = 32, 64, 80


class Gather:
    def __init__(self, slot, own, place, at, k, major, minor, sems):
        self.slot, self.own, self.place, self.at, self.k = slot, own, place, at, k
        self.m, self.n = major, minor
        self.send, self.recv, self.chip_send, self.chip_recv = sems
        self.sent = []

    def shard(self, dm, dn):
        return lax.rem(self.m + dm, 4) * 2 + (self.n if dn == 0 else 1 - self.n)

    def push(self, src, g, to):
        i = len(self.sent)
        copy = pltpu.make_async_remote_copy(
            src_ref=src,
            dst_ref=self.slot(self.k, g),
            send_sem=self.send.at[i],
            recv_sem=self.recv.at[g],
            device_id=self.at(to),
            device_id_type=MESH,
        )
        copy.start()
        self.sent.append(copy)

    def swap(self, src, g, sibling):
        pltpu.make_async_remote_copy(
            src_ref=src,
            dst_ref=self.slot(self.k, g),
            send_sem=self.chip_send.at[g],
            recv_sem=self.chip_recv.at[g],
            device_id=sibling,
            device_id_type=MESH,
        ).start()

    def wait(self, g):
        pltpu.make_async_remote_copy(
            src_ref=self.slot(self.k, g),
            dst_ref=self.slot(self.k, g),
            send_sem=self.send.at[0],
            recv_sem=self.recv.at[g],
            device_id=self.at(self.shard(0, 0)),
            device_id_type=MESH,
        ).wait_recv()

    def start(self, sibling):
        self.sibling = sibling
        me = self.shard(0, 0)
        self.push(self.own, me, self.shard(0, 1))
        self.push(self.own, me, self.shard(1, 0))
        self.push(self.own, me, self.shard(3, 0))
        self.swap(self.own, me, sibling)
        self.place(me)

    def pair(self):
        g = self.shard(0, 1)
        self.wait(g)
        self.push(self.slot(self.k, g), g, self.shard(1, 0))
        self.push(self.slot(self.k, g), g, self.shard(3, 0))
        self.swap(self.slot(self.k, g), g, self.sibling)

    def ring(self):
        g = self.shard(1, 0)
        self.wait(g)
        self.push(self.slot(self.k, g), g, self.shard(3, 0))
        self.swap(self.slot(self.k, g), g, self.sibling)
        g = self.shard(3, 0)
        self.wait(g)
        self.swap(self.slot(self.k, g), g, self.sibling)
        g = self.shard(3, 1)
        self.wait(g)
        self.push(self.slot(self.k, g), g, self.shard(1, 0))
        self.swap(self.slot(self.k, g), g, self.sibling)

    def rest(self):
        for dm, dn in ((1, 1), (2, 0), (2, 1)):
            g = self.shard(dm, dn)
            self.wait(g)
            self.swap(self.slot(self.k, g), g, self.sibling)

    def halves(self):
        for g in range(G):
            pltpu.make_async_remote_copy(
                src_ref=self.slot(1 - self.k, g),
                dst_ref=self.slot(1 - self.k, g),
                send_sem=self.chip_send.at[g],
                recv_sem=self.chip_recv.at[g],
                device_id=self.sibling,
                device_id_type=MESH,
            ).wait_recv()

    def drain(self):
        for copy in self.sent:
            copy.wait_send()
        for g in range(G):
            pltpu.make_async_remote_copy(
                src_ref=self.slot(self.k, g),
                dst_ref=self.slot(self.k, g),
                send_sem=self.chip_send.at[g],
                recv_sem=self.chip_recv.at[g],
                device_id=self.sibling,
                device_id_type=MESH,
            ).wait_send()


STEP = 4


def exchange_kernel(
    tab,
    mask_hbm,
    sib_cot_hbm,
    sib_panel_hbm,
    par_cot_hbm,
    par_panel_hbm,
    sib_hbm,
    par_hbm,
    part_out,
    lc_out,
    lp_out,
    sib_out,
    parg_out,
    mask,
    sib_cot,
    sib_panel,
    par_panel,
    sib_v,
    par_v,
    sc,
    pc,
    pp,
    mcol,
    halves,
    other,
    halves_p,
    other_p,
    chip_sib,
    chip_par,
    pieces,
    par_pieces,
    pack_cot,
    pack_pan,
    got_cot,
    got_pan,
    got_par,
    pt,
    ct,
    far,
    near_l,
    near_r,
    zs,
    zr,
    s_in,
    s_mid,
    s_last,
    pmat,
    tiles,
    ag_send,
    ag_recv,
    ag_cs,
    ag_cr,
    load_sem,
    place_sem,
    tile_sem,
    x_sem,
    b_send,
    b_recv,
    e_send,
    e_recv,
    c_send,
    c_recv,
    d_send,
    d_recv,
    f_send,
    f_recv,
    r_send,
    r_recv,
    q_send,
    q_recv,
):
    r = lax.axis_index("row")
    c = lax.axis_index("col")
    k = c % 2
    p = c // 2
    y, zh, x, zl = p // 2, p % 2, r // 2, r % 2
    sibling = (r, p * 2 + 1 - k)
    started = []

    def in_row(q):
        return (q, c)

    def in_col(q):
        return (r, q * 2 + k)

    def remote(src, dst, send, recv, to):
        return pltpu.make_async_remote_copy(
            src_ref=src, dst_ref=dst, send_sem=send, recv_sem=recv, device_id=to, device_id_type=MESH
        )

    def give(src, dst, send, recv, to):
        copy = remote(src, dst, send, recv, to)
        copy.start()
        started.append(copy)

    def take(dst, send, recv):
        remote(dst, dst, send, recv, sibling).wait_recv()

    def each(dst, at, me, send, recv):
        for d in range(1, G):
            g = lax.rem(me + d, G)
            take(dst.at[at(g)], send.at[d], recv.at[g])

    barrier = pltpu.get_barrier_semaphore()
    pl.semaphore_signal(barrier, inc=1, device_id=sibling, device_id_type=MESH)
    for d in range(1, G):
        pl.semaphore_signal(barrier, inc=1, device_id=in_row(lax.rem(r + d, G)), device_id_type=MESH)
        pl.semaphore_signal(barrier, inc=1, device_id=in_col(lax.rem(p + d, G)), device_id_type=MESH)
    loads = [
        pltpu.make_async_copy(src, dst, load_sem.at[i])
        for i, (src, dst) in enumerate(
            (
                (par_panel_hbm, par_panel),
                (par_cot_hbm, pc.at[c]),
                (mask_hbm, mask),
                (sib_cot_hbm, sib_cot),
                (sib_panel_hbm, sib_panel),
                (par_hbm, par_v),
                (sib_hbm, sib_v),
            )
        )
    ]
    for load in loads:
        load.start()

    def sems(i):
        return ag_send.at[i], ag_recv.at[i], ag_cs.at[i], ag_cr.at[i]

    def nothing(me):
        pass

    def placed(src, out, i):
        def place(me):
            pltpu.make_async_copy(src, out(k, me), place_sem.at[i]).start()

        return place

    def place_pp(me):
        pp[k, me] = got_par[...]

    def lc_slot(h, g):
        return lc_out.at[h, g]

    def lp_slot(h, g):
        return lp_out.at[h, g]

    ag_pc = Gather(lambda h, g: pc.at[g * 2 + h], pc.at[c], nothing, in_col, k, y, zh, sems(0))
    ag_sc = Gather(lambda h, g: sc.at[g * 2 + h], sc.at[c], nothing, in_col, k, y, zh, sems(1))
    ag_lc = Gather(lc_slot, got_cot, placed(got_cot, lc_slot, 0), in_col, k, y, zh, sems(2))
    ag_lp = Gather(lp_slot, got_pan, placed(got_pan, lp_slot, 1), in_row, k, x, zl, sems(3))
    ag_pp = Gather(lambda h, g: pp.at[h, g], got_par, place_pp, in_row, k, x, zl, sems(4))

    loads[0].wait()
    for h in range(2):
        halves_p[h] = par_panel[:, h * H : (h + 1) * H]
    loads[1].wait()
    pl.semaphore_wait(barrier, 2 * G - 1)
    give(halves_p.at[1 - k], other_p, x_sem.at[0], x_sem.at[1], sibling)
    ag_pc.start(sibling)

    for load in loads[2:5]:
        load.wait()
    line = (r * 16 + c) * 3 // 2
    for i in range(2):
        row = mask[pl.ds(line + i, 1), :].astype(jnp.float32)
        mcol[i * BLK : (i + 1) * BLK] = jnp.broadcast_to(row, (BLK, BLK)).T.astype(jnp.bfloat16)
    live = mcol[pl.ds(pl.multiple_of(k * 64, 64), SIB)]
    for h in range(2):
        for i in range(2):
            lanes = slice(h * H + i * BLK, h * H + (i + 1) * BLK)
            cot = sib_cot[:, lanes] * live
            sc[c, :, lanes] = cot
            halves[h, :SIB, i * BLK : (i + 1) * BLK] = cot
            halves[h, SIB:, i * BLK : (i + 1) * BLK] = sib_panel[:, lanes] * live
    give(halves.at[1 - k], other, x_sem.at[2], x_sem.at[3], sibling)

    def strip(i):
        return pl.ds(pl.multiple_of(i * PIECE, PIECE), PIECE)

    take(other_p, x_sem.at[0], x_sem.at[1])
    chip_par[k] = halves_p[k]
    chip_par[1 - k] = other_p[...]
    for d in range(1, G):
        to = lax.rem(r + d, G)
        give(chip_par.at[:, strip(to)], par_pieces.at[r], e_send.at[d], e_recv.at[r], in_row(to))
    par_pieces[r] = chip_par[:, strip(r)]

    take(other, x_sem.at[2], x_sem.at[3])
    first = k == 0
    for ch in range(2):
        mine, theirs = halves[k, ch * SIB : (ch + 1) * SIB], other[ch * SIB : (ch + 1) * SIB]
        low, high = jnp.where(first, mine, theirs), jnp.where(first, theirs, mine)
        chip_sib[ch, 0] = low[:BLK]
        chip_sib[ch, 1, : BLK // 2] = low[BLK:]
        chip_sib[ch, 1, BLK // 2 :] = high[: BLK // 2]
        chip_sib[ch, 2] = high[BLK // 2 :]
    for d in range(1, G):
        to = lax.rem(p + d, G)
        give(chip_sib.at[:, :, strip(to)], pieces.at[:, pl.ds(p * 3, 3)], b_send.at[d], b_recv.at[p], in_col(to))
    pieces[:, pl.ds(p * 3, 3)] = chip_sib[:, :, strip(p)]

    each(par_pieces, lambda g: g, r, e_send, e_recv)
    for d in range(1, G):
        to = lax.rem(p + d, G)
        give(par_pieces.at[to], got_par.at[p], f_send.at[d], f_recv.at[p], in_col(to))
    got_par[p] = par_pieces[p]

    ag_pc.pair()
    for d in range(1, G):
        g = lax.rem(p + d, G)
        take(pieces.at[:, pl.ds(g * 3, 3)], b_send.at[d], b_recv.at[g])

    @pl.loop(0, G)
    def _(q):
        for t in range(CAP):
            j = tab[q * CAP + t]
            pack_cot[q, t] = pieces[0, j]
            pack_pan[q, t] = pieces[1, j]

    for d in range(1, G):
        to = lax.rem(p + d, G)
        give(pack_pan.at[to], got_pan.at[p], d_send.at[d], d_recv.at[p], in_col(to))
    for d in range(1, G):
        to = lax.rem(r + d, G)
        give(pack_cot.at[to], got_cot.at[r], c_send.at[d], c_recv.at[r], in_row(to))
    got_pan[p] = pack_pan[p]
    got_cot[r] = pack_cot[r]

    each(got_par, lambda g: g, p, f_send, f_recv)
    ag_pp.start(sibling)
    ag_pc.ring()
    each(got_pan, lambda g: g, p, d_send, d_recv)
    ag_lp.start(sibling)
    each(got_cot, lambda g: g, r, c_send, c_recv)
    ag_lc.start(sibling)
    ag_pc.rest()
    ag_pp.pair()
    ag_pc.halves()

    loads[5].wait()
    rows_p = par_v.shape[0]

    @pl.loop(0, par_v.shape[1] // 256)
    def _(i):
        at = pl.ds(pl.multiple_of(i * 256, 256), 256)
        part = lax.dot_general(
            pc[...].reshape(rows_p, 2 * H), par_v[:, at], TN, preferred_element_type=jnp.float32
        )
        pt[:, :, at] = part.reshape(8, H // 4, 256)

    def piece(dm, dn):
        return lax.rem(x + dm, 4) * 2 + (zl if dn == 0 else 1 - zl)

    right, left, mate = in_row(piece(1, 0)), in_row(piece(3, 0)), in_row(piece(0, 1))

    def r_give(src, dst, i, to):
        give(src, dst, r_send.at[i], r_recv.at[i], to)

    def r_take(dst, i):
        take(dst, r_send.at[i], r_recv.at[i])

    def q_give(src, dst, i, to):
        give(src, dst, q_send.at[i], q_recv.at[i], to)

    def q_take(dst, i):
        take(dst, q_send.at[i], q_recv.at[i])

    r_give(pt.at[piece(2, 0)], far.at[0], 0, right)
    r_give(pt.at[piece(2, 1)], far.at[1], 1, left)
    r_give(pt.at[piece(1, 1)], near_l.at[1], 2, right)
    r_give(pt.at[piece(3, 0)], near_r.at[0], 3, left)

    ag_sc.start(sibling)
    ag_lp.pair()
    ag_lc.pair()
    ag_pp.ring()
    ag_sc.pair()

    r_take(far.at[0], 0)
    pt[piece(1, 0)] = pt[piece(1, 0)] + far[0]
    r_give(pt.at[piece(1, 0)], near_l.at[0], 4, right)
    r_take(far.at[1], 1)
    pt[piece(3, 1)] = pt[piece(3, 1)] + far[1]
    r_give(pt.at[piece(3, 1)], near_r.at[1], 5, left)

    ag_sc.ring()
    ag_lc.ring()
    ag_sc.rest()
    ag_sc.halves()

    loads[6].wait()
    rows_s, cols_s = sib_v.shape
    cut = cols_s // 3 * 2
    parts = (slice(0, cut), slice(cut, cols_s))
    xb = x % 2
    beside = in_row((x + 1 - 2 * xb) * 2 + zl)
    own, by_z, by_x, by_xz = xb * 2 + zl, xb * 2 + 1 - zl, (1 - xb) * 2 + zl, (1 - xb) * 2 + 1 - zl

    def sib_part(i):
        part = lax.dot_general(
            sc[...].reshape(rows_s, 2 * H), sib_v[:, parts[i]], TN, preferred_element_type=jnp.float32
        )
        ct[:, :, parts[i]] = part.reshape(4, H // 2, -1)

    r_take(near_l.at[1], 2)
    r_take(near_r.at[1], 5)
    zs[...] = pt[piece(0, 1)] + near_l[1] + near_r[1]
    r_give(zs, zr, 6, mate)

    sib_part(0)
    q_give(ct.at[by_xz, :, parts[0]], s_in.at[1, :, parts[0]], 0, mate)
    q_give(ct.at[by_z, :, parts[0]], s_in.at[0, :, parts[0]], 1, mate)
    sib_part(1)
    q_give(ct.at[by_xz, :, parts[1]], s_in.at[1, :, parts[1]], 2, beside)
    q_give(ct.at[by_x, :, parts[1]], s_in.at[0, :, parts[1]], 3, beside)

    ag_lp.ring()
    ag_pp.rest()
    q_take(s_in.at[1, :, parts[1]], 2)
    s_mid[:, parts[1]] = ct[by_z, :, parts[1]] + s_in[1, :, parts[1]]
    q_give(s_mid.at[:, parts[1]], s_last.at[:, parts[1]], 5, mate)
    q_take(s_in.at[1, :, parts[0]], 0)
    s_mid[:, parts[0]] = ct[by_x, :, parts[0]] + s_in[1, :, parts[0]]
    q_give(s_mid.at[:, parts[0]], s_last.at[:, parts[0]], 4, beside)

    ag_pp.halves()
    for n in range(8):
        rows = slice(n * BLK, (n + 1) * BLK)
        for h in range(2):
            pmat[rows, h * H : (h + 1) * H] = pp[h, :, 4 * k + n // 2, n % 2].reshape(BLK, H)
    rows_t = STEP * BLK
    stores = []

    def tile(t):
        if t >= 2:
            stores[t - 2].wait()
        tiles[t % 2] = lax.dot_general(
            pc[t * STEP : (t + 1) * STEP].reshape(rows_t, 2 * H),
            pmat[...],
            NT,
            preferred_element_type=jnp.float32,
        )
        stores.append(
            pltpu.make_async_copy(tiles.at[t % 2], part_out.at[t * rows_t : (t + 1) * rows_t], tile_sem.at[t % 2])
        )
        stores[t].start()

    tile(0)
    tile(1)
    tile(2)
    ag_lc.rest()
    ag_lp.rest()
    tile(3)

    r_take(near_l.at[0], 4)
    r_take(near_r.at[0], 3)
    r_take(zr, 6)
    parg_out[...] = -(pt[piece(0, 0)] + near_l[0] + near_r[0] + zr[...])
    q_take(s_in.at[0, :, parts[0]], 1)
    q_take(s_in.at[0, :, parts[1]], 3)
    q_take(s_last.at[:, parts[0]], 4)
    q_take(s_last.at[:, parts[1]], 5)
    first_line = (x // 2) * (mask.shape[0] // 2) + c * (cols_s // BLK)
    for j in range(cols_s // BLK):
        lanes = slice(j * BLK, (j + 1) * BLK)
        keep = mask[pl.ds(first_line + j, 1), :].astype(jnp.float32)
        sib_out[lanes, :] = (-(ct[own, :, lanes] + s_in[0, :, lanes] + s_last[:, lanes]) * keep).T

    ag_lc.halves()
    ag_lp.halves()

    for copy in started:
        copy.wait_send()
    for ag in (ag_pc, ag_sc, ag_lc, ag_lp, ag_pp):
        ag.drain()
    pltpu.make_async_copy(got_cot, lc_slot(k, p), place_sem.at[0]).wait()
    pltpu.make_async_copy(got_pan, lp_slot(k, r), place_sem.at[1]).wait()
    stores[-2].wait()
    stores[-1].wait()


def exchange(tab, mask, sib_cot, sib_panel, par_cot, par_panel, sib_inverse, par_inverse):
    bf, f32 = jnp.bfloat16, jnp.float32
    srows, scols = sib_inverse.shape
    prows, pcols = par_inverse.shape
    anyspace = pl.BlockSpec(memory_space=pl.ANY)
    vmem = pl.BlockSpec(memory_space=pltpu.VMEM)
    dma = pltpu.SemaphoreType.DMA
    lifted = jax.ShapeDtypeStruct((2, G, G, CAP, PIECE, H), bf)
    return pl.pallas_call(
        exchange_kernel,
        out_shape=(
            jax.ShapeDtypeStruct((prows, pcols), f32),
            lifted,
            lifted,
            jax.ShapeDtypeStruct((scols, H // 2), f32),
            jax.ShapeDtypeStruct((H // 4, pcols), f32),
        ),
        in_specs=[pl.BlockSpec(memory_space=pltpu.SMEM)] + [anyspace] * 7,
        out_specs=(anyspace, anyspace, anyspace, vmem, vmem),
        scratch_shapes=[
            pltpu.VMEM(mask.shape, jnp.int32),
            pltpu.VMEM((SIB, 2 * H), bf),
            pltpu.VMEM((SIB, 2 * H), bf),
            pltpu.VMEM((PAR, 2 * H), bf),
            pltpu.VMEM((srows, scols), bf),
            pltpu.VMEM((prows, pcols), bf),
            pltpu.VMEM((2 * G, SIB, 2 * H), bf),
            pltpu.VMEM((2 * G, PAR, 2 * H), bf),
            pltpu.VMEM((2, G, G, 2, PIECE, H), bf),
            pltpu.VMEM((2 * BLK, BLK), bf),
            pltpu.VMEM((2, 2 * SIB, H), bf),
            pltpu.VMEM((2 * SIB, H), bf),
            pltpu.VMEM((2, PAR, H), bf),
            pltpu.VMEM((PAR, H), bf),
            pltpu.VMEM((2, 3, BLK, H), bf),
            pltpu.VMEM((2, BLK, H), bf),
            pltpu.VMEM((2, 3 * G, PIECE, H), bf),
            pltpu.VMEM((G, 2, PIECE, H), bf),
            pltpu.VMEM((G, CAP, PIECE, H), bf),
            pltpu.VMEM((G, CAP, PIECE, H), bf),
            pltpu.VMEM((G, CAP, PIECE, H), bf),
            pltpu.VMEM((G, CAP, PIECE, H), bf),
            pltpu.VMEM((G, 2, PIECE, H), bf),
            pltpu.VMEM((8, H // 4, pcols), f32),
            pltpu.VMEM((4, H // 2, scols), f32),
            pltpu.VMEM((2, H // 4, pcols), f32),
            pltpu.VMEM((2, H // 4, pcols), f32),
            pltpu.VMEM((2, H // 4, pcols), f32),
            pltpu.VMEM((H // 4, pcols), f32),
            pltpu.VMEM((H // 4, pcols), f32),
            pltpu.VMEM((2, H // 2, scols), f32),
            pltpu.VMEM((H // 2, scols), f32),
            pltpu.VMEM((H // 2, scols), f32),
            pltpu.VMEM((pcols, 2 * H), bf),
            pltpu.VMEM((2, STEP * BLK, pcols), f32),
            dma((5, 8)),
            dma((5, 8)),
            dma((5, 8)),
            dma((5, 8)),
            dma((7,)),
            dma((2,)),
            dma((2,)),
            dma((4,)),
            *[dma((8,))] * 10,
            dma((7,)),
            dma((7,)),
            dma((6,)),
            dma((6,)),
        ],
        compiler_params=pltpu.CompilerParams(
            collective_id=0, has_side_effects=True, vmem_limit_bytes=54 << 20
        ),
    )(tab, mask, sib_cot, sib_panel, par_cot, par_panel, sib_inverse, par_inverse)


def border_kernel(tab, part, *refs):
    lifted, panels, (out, left, right) = refs[: 2 * STEP], refs[2 * STEP : 2 * STEP + 16], refs[2 * STEP + 16 :]
    i = pl.program_id(0)

    def lanes(s, h):
        return slice((2 * s + h) * H, (2 * s + h + 1) * H)

    @pl.when(i == 0)
    def _():
        for b in range(8):
            rows = slice(b * BLK, (b + 1) * BLK)
            for h in range(2):
                for s in range(2):
                    block = panels[s * 8 + b][h, 0, :, 0].reshape(BLK, H)
                    there = tab[COL_TAB + s * 8 + b] >= 0
                    right[rows, lanes(s, h)] = jnp.where(there, block, jnp.zeros_like(block))

    for b in range(STEP):
        rows = slice(b * BLK, (b + 1) * BLK)
        for s in range(2):
            there = tab[ROW_TAB + s * 16 + i * STEP + b] >= 0
            for h in range(2):
                block = lifted[s * STEP + b][h, :, 0].reshape(BLK, H)
                left[rows, lanes(s, h)] = jnp.where(there, block, jnp.zeros_like(block))
    out[...] = -(part[...] + lax.dot_general(left[...], right[...], NT, preferred_element_type=jnp.float32))


def border(tab, part, lc, lp):
    rows, cols = part.shape
    lc = lc.reshape(2, G, G * CAP, PIECE, H)

    def lifted_spec(s, b):
        return pl.BlockSpec(
            (2, G, 1, PIECE, H),
            lambda i, t: (0, 0, jnp.maximum(t[ROW_TAB + s * 16 + i * STEP + b], 0), 0, 0),
        )

    def panel_spec(n):
        def at(i, t):
            slot = jnp.maximum(t[COL_TAB + n], 0)
            return 0, slot // CAP, 0, slot % CAP, 0, 0

        return pl.BlockSpec((2, 1, G, 1, PIECE, H), at, pipeline_mode=pl.Buffered(1))

    return pl.pallas_call(
        border_kernel,
        out_shape=jax.ShapeDtypeStruct((rows, cols), jnp.float32),
        grid_spec=pltpu.PrefetchScalarGridSpec(
            num_scalar_prefetch=1,
            grid=(2 * G // STEP,),
            in_specs=[pl.BlockSpec((STEP * BLK, cols), lambda i, t: (i, 0))]
            + [lifted_spec(s, b) for s in range(2) for b in range(STEP)]
            + [panel_spec(n) for n in range(16)],
            out_specs=pl.BlockSpec((STEP * BLK, cols), lambda i, t: (i, 0)),
            scratch_shapes=[
                pltpu.VMEM((STEP * BLK, 4 * H), jnp.bfloat16),
                pltpu.VMEM((cols, 4 * H), jnp.bfloat16),
            ],
        ),
        compiler_params=pltpu.CompilerParams(vmem_limit_bytes=50 << 20),
    )(tab, part, *([lc] * (2 * STEP)), *([lp] * 16))


def tables(block_map, r, c):
    blocks = 3 * G
    tile_blocks = 2 * G
    ids = block_map.reshape(G, blocks)
    dest = ids // tile_blocks
    iota = jnp.arange(blocks, dtype=jnp.int32)
    tile = jnp.arange(G, dtype=jnp.int32)[:, None]
    before = (dest[:, :, None] == dest[:, None, :]) & (iota[None, None, :] < iota[None, :, None])
    rank = jnp.sum(before.astype(jnp.int32), axis=-1)
    n = jnp.arange(END, dtype=jnp.int32)[:, None, None]
    slot = dest * CAP + rank
    in_slot = (n < ROW_TAB) & (tile == r)[None] & (slot[None] == n)
    s, row_at, col_at = tile // (G // 2), n - ROW_TAB, n - COL_TAB
    in_rows = (n >= ROW_TAB) & (n < COL_TAB) & (s[None] == row_at // 16) & (ids[None] == r * 16 + row_at % 16)
    in_cols = (n >= COL_TAB) & (n < END) & (s[None] == col_at // 8) & (ids[None] == c * 8 + col_at % 8)
    value = jnp.where(in_slot, iota[None, None], 0) + jnp.where(in_rows | in_cols, (tile * CAP + rank + 1)[None], 0)
    flat = n[:, 0, 0]
    return jnp.sum(value, axis=(1, 2)) + jnp.where(flat < ROW_TAB, 0, -1)


def on_device(sib_inverse, sib_panel, sib_cot, par_inverse, par_panel, par_cot, block_map, row_mask):
    r = lax.axis_index("row")
    c = lax.axis_index("col")
    tab = tables(block_map, r, c)
    mask = row_mask.reshape(-1, BLK)
    part, lc, lp, sib_sum, par_sum = exchange(
        tab, mask, sib_cot, sib_panel, par_cot, par_panel, sib_inverse, par_inverse
    )
    return sib_sum, par_sum.T, border(tab, part, lc, lp)


def solution(mesh):
    placed = (
        P("row", "col"),
        P(("row", "col"), None),
        P(("row", "col"), None),
        P("row", "col"),
        P(("row", "col"), None),
        P(("row", "col"), None),
        P(),
        P(),
    )
    return jax.shard_map(
        on_device,
        mesh=mesh,
        in_specs=placed,
        out_specs=(P("col", "row"), P("col", "row"), P("row", "col")),
        check_vma=False,
    )
```
